32 devices in a mesh: grp: 2 (over y), doc: 4 (over x, core), voc: 4 (over z).
Axes of the slice: x: 2, y: 2, z: 4, core: 2. Of those that a mesh axis runs over, the one named last changes fastest.
Arguments:
- hidden: bfloat16 [48, 256, 768], P(('grp', 'doc')), parts along dimension 0, may hold values from -6 to 6
- lengths: int32 [48], P(('grp', 'doc')), parts along dimension 0, may hold values from 1 to 256, 3840 in all
- w_trans: bfloat16 [768, 768], replicated, may hold values from -0.21875 to 0.21875
- b_trans: float32 [768], replicated, may hold values from -3 to 3
- ln_gain: float32 [768], replicated, may hold values from 0.5 to 1.5
- ln_bias: float32 [768], replicated, may hold values from -3 to 3
- w_decode: bfloat16 [768, 30720], P(None, 'voc'), may hold values from -0.21875 to 0.21875
- b_decode: float32 [30720], P('voc'), may hold values from -5 to 5
- query_ids: int32 [2048, 32], P('grp'), parts along dimension 0, may hold values from 0 to 30719
- query_wts: int32 [2048, 32], P('grp'), parts along dimension 0, may hold values from 1 to 100
Outputs:
- scores: float32 [48, 1024], P(('grp', 'voc'), 'doc'), parts along dimension 0
The draws below stay inside these ranges and needn't reach their ends.
There are 2 independent parts, one for each index of `grp`. The reference program is written for one: setup_inputs(seed, part) draws one part's arguments, and reference() takes and returns one part's arrays. A program takes and returns all parts, laid end to end along the dimension named above; an argument that names none is the same for every part. Nothing has to cross between parts.
Inputs may be any that keep to these rules, and one draw needn't show every extreme that they name: Every passage has at least one live token and the longest has exactly 256. Within each grp group the 24 lengths sum to 3840; over the whole array, which holds both groups, the sum is twice that.
All inputs are finite; a program needn't handle non-finite values.
Results may differ from the reference program's by a relative error of at most 0.0003.
Values sent between devices are 32-bit elements; how exact they have to be, the bound alone decides.
A program may use at most 64 MiB of HBM per device.

```python
import math
import jax
import jax.numpy as jnp
import numpy as np
from jax import lax

D = 768
V = 30720
L = 256
QT = 32
P_SIZE = 24
Q = 1024


def plant(result, stream_key, smallest, largest):
    index_at = [jax.random.randint(jax.random.fold_in(stream_key, axis), (), 0, length) for axis, length in enumerate(result.shape)]
    main_axis = result.shape.index(max(result.shape))
    next_to = index_at[:main_axis] + [(index_at[main_axis] + 1) % result.shape[main_axis]] + index_at[main_axis + 1:]
    return result.at[tuple(index_at)].set(smallest).at[tuple(next_to)].set(largest)


def levels(stream_key, dims, cuts, least, top_value):
    gain, own = 1.0, jax.random.fold_in(stream_key, 6)
    for position, parts in cuts:
        steps = jnp.exp(jax.random.uniform(jax.random.fold_in(own, position), (parts,), jnp.float32, least / len(cuts), top_value / len(cuts)))
        gain = gain * jnp.repeat(steps, dims[position] // parts).reshape([-1 if axis == position else 1 for axis in range(len(dims))])
    return gain


def length_profile(number_of, total, limit, lean):
    loads = [(1 << 20) // math.isqrt(standing ** lean) + 1 for standing in range(2, number_of + 1)]
    spare, counts = total - limit - (number_of - 1), [1] * (number_of - 1)
    while spare > 0:
        free = [i for i in range(number_of - 1) if counts[i] < limit]
        pool, budget = sum([loads[i] for i in free]), spare
        for i in free:
            extra = min(limit - counts[i], max(1, budget * loads[i] // pool), spare)
            counts[i] = counts[i] + extra
            spare = spare - extra
    return np.array([limit] + counts)


def ragged(own_key, count, total, reach, lean):
    if count == 2:
        one = jax.random.randint(own_key, (), max(1, total - reach), min(reach, total - 1) + 1)
        return jnp.stack([one, total - one])
    sizes = jnp.asarray(length_profile(count, total, reach, lean), jnp.int32)
    twos = (count - 1) // 2
    source_of, sink = sizes[1:1 + 2 * twos:2], sizes[2:2 + 2 * twos:2]
    slack = jnp.minimum(source_of - 1, reach - sink)
    moved = jax.random.randint(jax.random.fold_in(own_key, 1), (twos,), 0, 1 << 20) % (slack + 1)
    sizes = sizes.at[1:1 + 2 * twos:2].set(source_of - moved).at[2:2 + 2 * twos:2].set(sink + moved)
    return sizes[jax.random.permutation(jax.random.fold_in(own_key, 2), count)]


def gaussian(stream_key, shape, scale, bound, shards=(), held_as=jnp.bfloat16):
    result = jax.random.normal(stream_key, shape, jnp.float32) * scale
    if len(shards) > 0:
        result = levels(stream_key, shape, shards, -0.22, 0.18) * result
    return jnp.clip(result, min=-bound, max=bound).astype(held_as)


def setup_inputs(seed: int = 0, part: int = 0) -> dict:
    splits = jax.random.split(jax.random.key(seed), 11)
    part_keys = jax.random.split(jax.random.fold_in(splits[10], part), 11)
    return {
        "hidden": gaussian(part_keys[0], (P_SIZE, L, D), 1.0, 6.0, ((0, 4),)),
        "lengths": ragged(part_keys[1], P_SIZE, P_SIZE * L * 5 // 8, L, 1).astype(jnp.int32),
        "w_trans": gaussian(splits[2], (D, D), D ** -0.5, 0.21875),
        "b_trans": gaussian(splits[3], (D,), 0.5, 3.0, (), jnp.float32),
        "ln_gain": jnp.clip(jax.random.uniform(splits[4], (D,), jnp.float32, 0.5, 1.5), 0.5, 1.5),
        "ln_bias": gaussian(splits[5], (D,), 0.5, 3.0, (), jnp.float32),
        "w_decode": gaussian(splits[6], (D, V), D ** -0.5, 0.21875, ((1, 4),)),
        "b_decode": gaussian(splits[7], (V,), 1.0, 5.0, ((0, 4),), jnp.float32),
        "query_ids": plant(jax.random.randint(part_keys[8], (Q, QT), 0, V), jax.random.fold_in(part_keys[8], 1), 0, V - 1).astype(jnp.int32),
        "query_wts": plant(jax.random.randint(part_keys[9], (Q, QT), 1, 101), jax.random.fold_in(part_keys[9], 1), 1, 100).astype(jnp.int32),
    }


eps = 1e-06
score_scale = 1.0 / 1024.0
dead_fill = -1e+30

def transform(hidden, w_trans, b_trans, ln_gain, ln_bias):
    count, length, width = hidden.shape
    flat = hidden.reshape(count * length, width)
    pre = jnp.dot(flat, w_trans, preferred_element_type=jnp.float32) + b_trans
    active = jax.nn.gelu(pre, approximate=False)
    centre = active - lax.optimization_barrier(jnp.mean(active, -1, keepdims=True))
    spread = lax.optimization_barrier(jnp.mean(centre * centre, -1, keepdims=True))
    normed = centre * lax.rsqrt(spread + eps) * ln_gain + ln_bias
    return normed.astype(jnp.bfloat16).reshape(count, length, width)

def reference(hidden, lengths, w_trans, b_trans, ln_gain, ln_bias, w_decode, b_decode, query_ids, query_wts):
    transformed = transform(hidden, w_trans, b_trans, ln_gain, ln_bias)
    decode_full = w_decode.astype(jnp.float32)

    def pool_rows(pair):
        passage, live = pair
        logits = jnp.dot(passage.astype(jnp.float32), decode_full) + b_decode
        inside = jnp.arange(passage.shape[0], dtype=jnp.int32)[:, None] < live
        top = lax.optimization_barrier(jnp.max(jnp.where(inside, logits, jnp.full_like(logits, dead_fill)), 0))
        return jnp.log1p(jnp.maximum(top, jnp.zeros_like(top)))
    impacts = lax.map(pool_rows, (transformed, lengths))
    weights = query_wts.astype(jnp.float32)
    picked = impacts[:, query_ids]
    return lax.optimization_barrier(jnp.sum(picked * weights[None], -1)) * score_scale
```

```python
import functools

import jax
import jax.numpy as jnp
from jax import lax
from jax.experimental import pallas as pl
from jax.experimental.pallas import tpu as pltpu
from jax.sharding import PartitionSpec as P

eps = 1e-06
score_scale = 1.0 / 1024.0
group = 16
chunk = 256


def pool_kernel(
    count, length, lens, hidden, w_trans, b_trans, gain, bias, w_decode, b_decode, out,
    kept, gathered, maxima, source, first
):
    per_chunk = chunk // group
    width = w_decode.shape[1]

    @pl.when(pl.program_id(0) == 0)
    def _():
        at = jnp.int32(0)
        for p in range(count):
            first[p] = at
            groups = (lens[p] + (group - 1)) // group

            def put(j, _, p=p, at=at):
                source[at + j] = p * length + j * group
                return 0

            lax.fori_loop(0, groups, put, 0)
            at = at + groups
        first[count] = at
        chunks = (at + (per_chunk - 1)) // per_chunk

        def pad(j, _):
            source[j] = 0
            return 0

        lax.fori_loop(at, chunks * per_chunk, pad, 0)

        def transform(c, _):
            for i in range(per_chunk):
                start = pl.multiple_of(source[c * per_chunk + i], group)
                gathered[i * group:(i + 1) * group, :] = hidden[pl.ds(start, group), :]
            pre = jnp.dot(gathered[...], w_trans[...], preferred_element_type=jnp.float32)
            pre = pre + b_trans[...]
            active = 0.5 * pre * (1.0 + lax.erf(pre * (0.5 ** 0.5)))
            centre = active - jnp.mean(active, -1, keepdims=True)
            spread = jnp.mean(centre * centre, -1, keepdims=True)
            normed = centre * lax.rsqrt(spread + eps) * gain[...] + bias[...]
            kept[pl.ds(pl.multiple_of(c * chunk, chunk), chunk), :] = normed.astype(jnp.bfloat16)
            return 0

        lax.fori_loop(0, chunks, transform, 0)
        for p in range(count):
            last = first[p + 1] - 1
            live = lens[p] - (last - first[p]) * group
            rows = pl.ds(pl.multiple_of(last * group, group), group)
            head = kept[pl.ds(pl.multiple_of(first[p] * group, group), group), :]
            head = head.astype(jnp.float32)[0:1, :]
            inside = lax.broadcasted_iota(jnp.int32, (group, kept.shape[1]), 0) < live
            fixed = jnp.where(inside, kept[rows, :].astype(jnp.float32), head)
            kept[rows, :] = fixed.astype(jnp.bfloat16)

    chunks = (first[count] + (per_chunk - 1)) // per_chunk

    def decode(c, _):
        rows = kept[pl.ds(pl.multiple_of(c * chunk, chunk), chunk), :]
        logits = jnp.dot(rows, w_decode[...], preferred_element_type=jnp.float32)
        tops = jnp.max(logits.reshape(per_chunk, group // 8, 8, width), 1)
        maxima[pl.ds(c * per_chunk, per_chunk)] = tops
        return 0

    lax.fori_loop(0, chunks, decode, 0)
    step = 4
    for p in range(count):
        start, last = first[p], first[p + 1] - 1

        def fold(j, top, start=start, last=last):
            for i in range(step):
                top = jnp.maximum(top, maxima[jnp.minimum(start + j * step + i, last)])
            return top

        trips = (last - start + step) // step
        top = lax.fori_loop(0, trips, fold, maxima[start])
        best = jnp.max(top, 0, keepdims=True) + b_decode[...]
        out[p:p + 1, :] = jnp.log1p(jnp.maximum(best, 0.0))


def tile_of(width):
    best = 128
    for tile in range(128, 1537, 128):
        if width % tile == 0:
            best = tile
    return best


def pool(hidden, lengths, w_trans, b_trans, ln_gain, ln_bias, w_decode, b_decode):
    count, length, features = hidden.shape
    terms = w_decode.shape[1]
    tile = tile_of(terms)
    rows = -(-count * length // chunk) * chunk
    whole = lambda shape: pl.BlockSpec(shape, lambda i, lens: (0, 0), pipeline_mode=pl.Buffered(1))
    return pl.pallas_call(
        functools.partial(pool_kernel, count, length),
        out_shape=jax.ShapeDtypeStruct((count, terms), jnp.float32),
        grid_spec=pltpu.PrefetchScalarGridSpec(
            num_scalar_prefetch=1,
            grid=(terms // tile,),
            in_specs=[
                whole((count * length, features)),
                whole((features, features)),
                whole((1, features)),
                whole((1, features)),
                whole((1, features)),
                pl.BlockSpec((features, tile), lambda i, lens: (0, i)),
                pl.BlockSpec((1, tile), lambda i, lens: (0, i)),
            ],
            out_specs=pl.BlockSpec((count, tile), lambda i, lens: (0, i)),
            scratch_shapes=[
                pltpu.VMEM((rows, features), jnp.bfloat16),
                pltpu.VMEM((chunk, features), jnp.bfloat16),
                pltpu.VMEM((rows // group, 8, tile), jnp.float32),
                pltpu.SMEM((rows // group,), jnp.int32),
                pltpu.SMEM((count + 1,), jnp.int32),
            ],
        ),
        compiler_params=pltpu.CompilerParams(
            dimension_semantics=("arbitrary",), vmem_limit_bytes=60 * 1024 * 1024
        ),
    )(
        lengths, hidden.reshape(count * length, features), w_trans, b_trans[None],
        ln_gain[None], ln_bias[None], w_decode, b_decode[None]
    )


def block_terms(query_ids, query_wts, start, width):
    local_ids = query_ids - start
    inside = (local_ids >= 0) & (local_ids < width)
    clipped = jnp.clip(local_ids, 0, width - 1)
    weights = jnp.where(inside, query_wts, 0).astype(jnp.float32)
    return (clipped, weights)


def score_rows(rows, local_ids, weights):
    picked = rows[:, local_ids]
    return jnp.sum(picked * weights[None], -1) * score_scale


def shards(
    hidden, lengths, w_trans, b_trans, ln_gain, ln_bias, w_decode, b_decode, query_ids, query_wts
):
    impacts = pool(hidden, lengths, w_trans, b_trans, ln_gain, ln_bias, w_decode, b_decode)
    term_width = w_decode.shape[1]
    term_start = lax.axis_index("voc") * term_width
    local_ids, weights = block_terms(query_ids, query_wts, term_start, term_width)
    own_count = query_ids.shape[0] // lax.axis_size("doc")
    own_start = lax.axis_index("doc") * own_count
    own_ids = lax.dynamic_slice_in_dim(local_ids, own_start, own_count, 0)
    own_weights = lax.dynamic_slice_in_dim(weights, own_start, own_count, 0)
    partial_value = score_rows(
        lax.all_gather(impacts, "doc", axis=0, tiled=True), own_ids, own_weights
    )
    return lax.psum_scatter(partial_value, "voc", scatter_dimension=0, tiled=True)


def solution(mesh):
    return jax.shard_map(
        shards,
        mesh=mesh,
        in_specs=(
            P(("grp", "doc"), None, None),
            P(("grp", "doc")),
            P(),
            P(),
            P(),
            P(),
            P(None, "voc"),
            P("voc"),
            P("grp", None),
            P("grp", None),
        ),
        out_specs=P(("grp", "voc"), "doc"),
        check_vma=False,
    )
```

```python
import functools

import jax
import jax.numpy as jnp
from jax import lax
from jax.experimental import pallas as pl
from jax.experimental.pallas import tpu as pltpu
from jax.sharding import PartitionSpec as P

eps = 1e-06
score_scale = 1.0 / 1024.0
group = 16
chunk = 256


def pool_kernel(
    count, length, lens, hidden, w_trans, b_trans, gain, bias, w_decode, b_decode, out,
    kept, gathered, maxima, source, first
):
    per_chunk = chunk // group
    width = w_decode.shape[1]

    @pl.when(pl.program_id(0) == 0)
    def _():
        at = jnp.int32(0)
        for p in range(count):
            first[p] = at
            groups = (lens[p] + (group - 1)) // group

            def put(j, _, p=p, at=at):
                source[at + j] = p * length + j * group
                return 0

            lax.fori_loop(0, groups, put, 0)
            at = at + groups
        first[count] = at
        chunks = (at + (per_chunk - 1)) // per_chunk

        def pad(j, _):
            source[j] = 0
            return 0

        lax.fori_loop(at, chunks * per_chunk, pad, 0)

        def transform(c, _):
            for i in range(per_chunk):
                start = pl.multiple_of(source[c * per_chunk + i], group)
                gathered[i * group:(i + 1) * group, :] = hidden[pl.ds(start, group), :]
            pre = jnp.dot(gathered[...], w_trans[...], preferred_element_type=jnp.float32)
            pre = pre + b_trans[...][None]
            active = 0.5 * pre * (1.0 + lax.erf(pre * (0.5 ** 0.5)))
            centre = active - jnp.mean(active, -1, keepdims=True)
            spread = jnp.mean(centre * centre, -1, keepdims=True)
            normed = centre * lax.rsqrt(spread + eps) * gain[...][None] + bias[...][None]
            kept[pl.ds(pl.multiple_of(c * chunk, chunk), chunk), :] = normed.astype(jnp.bfloat16)
            return 0

        lax.fori_loop(0, chunks, transform, 0)
        for p in range(count):
            last = first[p + 1] - 1
            live = lens[p] - (last - first[p]) * group
            rows = pl.ds(pl.multiple_of(last * group, group), group)
            head = kept[pl.ds(pl.multiple_of(first[p] * group, group), group), :]
            head = head.astype(jnp.float32)[0:1, :]
            inside = lax.broadcasted_iota(jnp.int32, (group, kept.shape[1]), 0) < live
            fixed = jnp.where(inside, kept[rows, :].astype(jnp.float32), head)
            kept[rows, :] = fixed.astype(jnp.bfloat16)

    chunks = (first[count] + (per_chunk - 1)) // per_chunk

    def decode(c, _):
        rows = kept[pl.ds(pl.multiple_of(c * chunk, chunk), chunk), :]
        logits = jnp.dot(rows, w_decode[...], preferred_element_type=jnp.float32)
        tops = jnp.max(logits.reshape(per_chunk, group // 8, 8, width), 1)
        maxima[pl.ds(c * per_chunk, per_chunk)] = tops
        return 0

    lax.fori_loop(0, chunks, decode, 0)
    offset = pl.multiple_of(pl.program_id(0) * width, width)
    term_bias = b_decode[pl.ds(offset, width)][None]
    step = 4
    for p in range(count):
        start, last = first[p], first[p + 1] - 1

        def fold(j, top, start=start, last=last):
            for i in range(step):
                top = jnp.maximum(top, maxima[jnp.minimum(start + j * step + i, last)])
            return top

        trips = (last - start + step) // step
        top = lax.fori_loop(0, trips, fold, maxima[start])
        best = jnp.max(top, 0, keepdims=True) + term_bias
        out[p:p + 1, :] = jnp.log1p(jnp.maximum(best, 0.0))


def tile_of(width):
    best = 128
    for tile in range(128, 1537, 128):
        if width % tile == 0:
            best = tile
    return best


def pool(hidden, lengths, w_trans, b_trans, ln_gain, ln_bias, w_decode, b_decode):
    count, length, features = hidden.shape
    terms = w_decode.shape[1]
    tile = tile_of(terms)
    rows = -(-count * length // chunk) * chunk
    whole = lambda shape: pl.BlockSpec(shape, lambda i, lens: (0, 0), pipeline_mode=pl.Buffered(1))
    vector = pl.BlockSpec((features,), lambda i, lens: (0,), pipeline_mode=pl.Buffered(1))
    return pl.pallas_call(
        functools.partial(pool_kernel, count, length),
        out_shape=jax.ShapeDtypeStruct((count, terms), jnp.float32),
        grid_spec=pltpu.PrefetchScalarGridSpec(
            num_scalar_prefetch=1,
            grid=(terms // tile,),
            in_specs=[
                whole((count * length, features)),
                whole((features, features)),
                vector, vector, vector,
                pl.BlockSpec((features, tile), lambda i, lens: (0, i)),
                pl.BlockSpec((terms,), lambda i, lens: (0,), pipeline_mode=pl.Buffered(1)),
            ],
            out_specs=pl.BlockSpec((count, tile), lambda i, lens: (0, i)),
            scratch_shapes=[
                pltpu.VMEM((rows, features), jnp.bfloat16),
                pltpu.VMEM((chunk, features), jnp.bfloat16),
                pltpu.VMEM((rows // group, 8, tile), jnp.float32),
                pltpu.SMEM((rows // group,), jnp.int32),
                pltpu.SMEM((count + 1,), jnp.int32),
            ],
        ),
        compiler_params=pltpu.CompilerParams(
            dimension_semantics=("arbitrary",), vmem_limit_bytes=60 * 1024 * 1024
        ),
    )(
        lengths, hidden.reshape(count * length, features), w_trans, b_trans, ln_gain, ln_bias,
        w_decode, b_decode
    )


radix = 256
pad = 8


def score_kernel(
    sizes, impacts, ids, wts, out,
    slots, own_ids, own_wts, hi_at, lo_at, weight_at, table, part, parts,
    load_sem, local_sem, doc_send, doc_recv, pass_send, pass_recv, voc_send, voc_recv
):
    docs, vocs = sizes
    count, width = impacts.shape
    slots_per, queries = own_ids.shape
    per = radix // slots_per
    leads = width // radix
    grp, doc, voc = (lax.axis_index(name) for name in ("grp", "doc", "voc"))
    mesh_ids = pl.DeviceIdType.MESH
    partner = doc + 1 - 2 * lax.rem(doc, 2)

    rows = pl.ds(pl.multiple_of(doc * queries, queries), queries)
    loads = [
        pltpu.make_async_copy(ids.at[:, rows], own_ids, load_sem.at[0]),
        pltpu.make_async_copy(wts.at[:, rows], own_wts, load_sem.at[1]),
    ]
    for load in loads:
        load.start()
    slots[:, count:, :] = jnp.zeros((docs, pad - count, width), jnp.float32)

    barrier = pltpu.get_barrier_semaphore()
    near = [(grp, lax.rem(doc + 2 * j, docs), voc) for j in range(1, docs // 2)]
    near.append((grp, partner, voc))
    along = [(grp, doc, lax.rem(voc + j, vocs)) for j in range(1, vocs)]
    for peer in near + along:
        pl.semaphore_signal(barrier, inc=1, device_id=peer, device_id_type=mesh_ids)
    pl.semaphore_wait(barrier, len(near) + len(along))

    live = pl.ds(0, count)
    sends = []
    for j, peer in enumerate(near):
        copy = pltpu.make_async_remote_copy(
            src_ref=impacts, dst_ref=slots.at[doc, live], send_sem=doc_send.at[j],
            recv_sem=doc_recv.at[j], device_id=peer, device_id_type=mesh_ids
        )
        copy.start()
        sends.append(copy)
    keep = pltpu.make_async_copy(impacts, slots.at[doc, live], local_sem)
    keep.start()

    for load in loads:
        load.wait()
    local = own_ids[...] - voc * width
    lead = jnp.clip(local >> 8, -1, leads)
    spread_to = (
        lax.broadcasted_iota(jnp.int32, (slots_per, radix), 1) % slots_per
        == lax.broadcasted_iota(jnp.int32, (slots_per, radix), 0)
    ).astype(jnp.float32).astype(jnp.bfloat16)

    def widen(value):
        value = value.astype(jnp.float32).astype(jnp.bfloat16)
        return lax.dot_general(
            value, spread_to, (((0,), (0,)), ((), ())), preferred_element_type=jnp.float32
        )

    own = (
        lax.broadcasted_iota(jnp.int32, (queries, radix), 0) % per
        == lax.broadcasted_iota(jnp.int32, (queries, radix), 1) // slots_per
    )
    hi_at[...] = jnp.where(own, widen(lead), -1.0)
    lo_at[...] = jnp.where(own, widen(local & (radix - 1)), 0.0)
    weight_at[...] = widen(own_wts[...])

    def build(g, _):
        at = pl.ds(pl.multiple_of(g * per, per), per)
        high, weight = hi_at[at, :], weight_at[at, :]
        low = jnp.sum(lo_at[at, :], 0, keepdims=True)
        spans = leads + leads % 2
        left = jnp.concatenate(
            [jnp.where(high == float(i), weight, 0.0) for i in range(spans)], 0
        ).astype(jnp.bfloat16)
        digits = lax.broadcasted_iota(jnp.int32, (radix, radix), 0).astype(jnp.float32)
        right = jnp.where(digits == low, 1.0, 0.0).astype(jnp.bfloat16)
        made = lax.dot_general(
            left, right, (((1,), (1,)), ((), ())), preferred_element_type=jnp.float32
        )
        for i in range(leads):
            table[at, i * radix:(i + 1) * radix] = made[i * per:(i + 1) * per]
        return 0

    groups = queries // per
    early = groups * 3 // 4
    lax.fori_loop(0, early, build, 0)
    for copy in sends:
        copy.wait()
    passed = []
    for j in range(1, docs // 2):
        held = slots.at[lax.rem(doc + docs - 2 * j, docs), live]
        copy = pltpu.make_async_remote_copy(
            src_ref=held, dst_ref=held, send_sem=pass_send.at[j - 1],
            recv_sem=pass_recv.at[j - 1], device_id=(grp, partner, voc), device_id_type=mesh_ids
        )
        copy.start()
        passed.append(copy)
    lax.fori_loop(early, groups, build, 0)
    keep.wait()
    for copy in passed:
        copy.wait()

    total = jnp.zeros((2 * docs * pad, queries), jnp.float32)
    step = width // 5
    for i in range(width // step):
        cut = slice(i * step, (i + 1) * step)
        value = slots[:, :, cut].reshape(docs * pad, step)
        top = value.astype(jnp.bfloat16)
        rest = (value - top.astype(jnp.float32)).astype(jnp.bfloat16)
        pair = jnp.concatenate([top, rest], 0)
        weight = table[:, cut]
        big = weight.astype(jnp.bfloat16)
        small = (weight - big.astype(jnp.float32)).astype(jnp.bfloat16)
        for piece in (big, small):
            total = total + lax.dot_general(
                pair, piece, (((1,), (1,)), ((), ())), preferred_element_type=jnp.float32
            )
    total = (total[:docs * pad] + total[docs * pad:]) * score_scale
    part[...] = total.reshape(docs, pad, queries)

    share = docs // vocs
    copies = []
    for j, peer in enumerate(along):
        copy = pltpu.make_async_remote_copy(
            src_ref=part.at[pl.ds(peer[2] * share, share)], dst_ref=parts.at[j],
            send_sem=voc_send.at[j], recv_sem=voc_recv.at[j], device_id=peer,
            device_id_type=mesh_ids
        )
        copy.start()
        copies.append(copy)
    result = part[pl.ds(voc * share, share)]
    for j, copy in enumerate(copies):
        copy.wait()
        result = result + parts[j]
    for i in range(share):
        out[i * count:(i + 1) * count, :] = result[i, :count]


def score(impacts, ids, wts):
    docs, vocs = lax.axis_size("doc"), lax.axis_size("voc")
    count, width = impacts.shape
    queries = ids.shape[1] // docs
    anywhere = pl.BlockSpec(memory_space=pl.ANY)
    inside = pl.BlockSpec(memory_space=pltpu.VMEM)
    lanes = pltpu.VMEM((queries, radix), jnp.float32)
    several = lambda n: pltpu.SemaphoreType.DMA((max(n, 1),))
    return pl.pallas_call(
        functools.partial(score_kernel, (docs, vocs)),
        out_shape=jax.ShapeDtypeStruct((docs * count // vocs, queries), jnp.float32),
        in_specs=[inside, anywhere, anywhere],
        out_specs=inside,
        scratch_shapes=[
            pltpu.VMEM((docs, pad, width), jnp.float32),
            pltpu.VMEM((ids.shape[0], queries), jnp.int32),
            pltpu.VMEM((ids.shape[0], queries), jnp.int32),
            lanes, lanes, lanes,
            pltpu.VMEM((queries, width), jnp.float32),
            pltpu.VMEM((docs, pad, queries), jnp.float32),
            pltpu.VMEM((vocs - 1, docs // vocs, pad, queries), jnp.float32),
            several(2), pltpu.SemaphoreType.DMA,
            several(docs // 2), several(docs // 2),
            several(docs // 2 - 1), several(docs // 2 - 1),
            several(vocs - 1), several(vocs - 1),
        ],
        compiler_params=pltpu.CompilerParams(
            collective_id=0, has_side_effects=True, vmem_limit_bytes=60 * 1024 * 1024
        ),
    )(impacts, ids, wts)


def shards(
    hidden, lengths, w_trans, b_trans, ln_gain, ln_bias, w_decode, b_decode, query_ids, query_wts
):
    impacts = pool(hidden, lengths, w_trans, b_trans, ln_gain, ln_bias, w_decode, b_decode)
    return score(impacts, query_ids.T, query_wts.T)


def solution(mesh):
    return jax.shard_map(
        shards,
        mesh=mesh,
        in_specs=(
            P(("grp", "doc"), None, None),
            P(("grp", "doc")),
            P(),
            P(),
            P(),
            P(),
            P(None, "voc"),
            P("voc"),
            P("grp", None),
            P("grp", None),
        ),
        out_specs=P(("grp", "voc"), "doc"),
        check_vma=False,
    )
```

```python
import functools

import jax
import jax.numpy as jnp
from jax import lax
from jax.experimental import pallas as pl
from jax.experimental.pallas import tpu as pltpu
from jax.sharding import PartitionSpec as P

eps = 1e-06
score_scale = 1.0 / 1024.0
radix = 256
pad = 8


def tile_of(width):
    best = 128
    for tile in range(128, 1537, 128):
        if width % tile == 0:
            best = tile
    return best


def encode_kernel(
    sizes, count, tile, lens, b_trans, gain, bias, b_decode, hidden, w_trans, w_decode, ids, wts,
    out, states, mix, decoder, kept, slots, own_ids, own_wts, hi_at, lo_at, weight_at, table,
    part, parts, load_sem, state_sem, decoder_sem, doc_send, doc_recv, voc_send, voc_recv
):
    docs, vocs = sizes
    length, features = hidden.shape[0] // count, hidden.shape[1]
    width = w_decode.shape[1]
    tiles = width // tile
    slots_per, queries = own_ids.shape
    per = radix // slots_per
    leads = width // radix
    grp, doc, voc = (lax.axis_index(name) for name in ("grp", "doc", "voc"))
    mesh_ids = pl.DeviceIdType.MESH

    def state_load(p):
        rows = pl.ds(pl.multiple_of(p * length, length), length)
        return pltpu.make_async_copy(hidden.at[rows], states.at[rows], state_sem.at[p])

    def decoder_load(t):
        cut = pl.ds(pl.multiple_of(t * tile, tile), tile)
        return pltpu.make_async_copy(w_decode.at[:, cut], decoder.at[t], decoder_sem.at[t])

    mix_load = pltpu.make_async_copy(w_trans, mix, load_sem.at[0])
    mix_load.start()
    for p in range(count):
        state_load(p).start()
    rows = pl.ds(pl.multiple_of(doc * queries, queries), queries)
    loads = [
        pltpu.make_async_copy(ids.at[:, rows], own_ids, load_sem.at[1]),
        pltpu.make_async_copy(wts.at[:, rows], own_wts, load_sem.at[2]),
    ]
    for load in loads:
        load.start()
    for t in range(tiles):
        decoder_load(t).start()

    barrier = pltpu.get_barrier_semaphore()
    across = [(grp, lax.rem(doc + j, docs), voc) for j in range(1, docs)]
    along = [(grp, doc, lax.rem(voc + j, vocs)) for j in range(1, vocs)]
    for peer in across + along:
        pl.semaphore_signal(barrier, inc=1, device_id=peer, device_id_type=mesh_ids)
    mix_load.wait()

    def transform(p, _):
        state_load(p).wait()
        rows = pl.ds(pl.multiple_of(p * length, length), length)
        pre = jnp.dot(states[rows, :], mix[...], preferred_element_type=jnp.float32)
        pre = pre + b_trans[...][None]
        active = 0.5 * pre * (1.0 + lax.erf(pre * (0.5 ** 0.5)))
        centre = active - jnp.mean(active, -1, keepdims=True)
        spread = jnp.mean(centre * centre, -1, keepdims=True)
        normed = centre * lax.rsqrt(spread + eps) * gain[...][None] + bias[...][None]
        inside = lax.broadcasted_iota(jnp.int32, (length, features), 0) < lens[p]
        kept[rows, :] = jnp.where(inside, normed, normed[0:1]).astype(jnp.bfloat16)
        return 0

    lax.fori_loop(0, count, transform, 0)
    pl.semaphore_wait(barrier, len(across) + len(along))

    def share_copy(j, t):
        mine = slots.at[doc, t]
        return pltpu.make_async_remote_copy(
            src_ref=mine, dst_ref=mine, send_sem=doc_send.at[j, t], recv_sem=doc_recv.at[j, t],
            device_id=across[j], device_id_type=mesh_ids
        )

    def decode(t, _):
        decoder_load(t).wait()
        tops = []
        for p in range(count):
            logits = jnp.dot(
                kept[p * length:(p + 1) * length, :], decoder[t],
                preferred_element_type=jnp.float32
            )
            tops.append(jnp.max(logits, 0, keepdims=True))
        tops.append(jnp.zeros((pad - count, tile), jnp.float32))
        cut = pl.ds(pl.multiple_of(t * tile, tile), tile)
        best = jnp.concatenate(tops, 0) + b_decode[cut][None]
        slots[doc, t] = jnp.log1p(jnp.maximum(best, 0.0))
        for j in range(len(across)):
            share_copy(j, t).start()
        return 0

    lax.fori_loop(0, tiles, decode, 0)

    for load in loads:
        load.wait()
    local = own_ids[...] - voc * width
    lead = jnp.clip(local >> 8, -1, leads)
    spread_to = (
        lax.broadcasted_iota(jnp.int32, (slots_per, radix), 1) % slots_per
        == lax.broadcasted_iota(jnp.int32, (slots_per, radix), 0)
    ).astype(jnp.float32).astype(jnp.bfloat16)

    def widen(value):
        value = value.astype(jnp.float32).astype(jnp.bfloat16)
        return lax.dot_general(
            value, spread_to, (((0,), (0,)), ((), ())), preferred_element_type=jnp.float32
        )

    own = (
        lax.broadcasted_iota(jnp.int32, (queries, radix), 0) % per
        == lax.broadcasted_iota(jnp.int32, (queries, radix), 1) // slots_per
    )
    hi_at[...] = jnp.where(own, widen(lead), -1.0)
    lo_at[...] = jnp.where(own, widen(local & (radix - 1)), 0.0)
    weight_at[...] = widen(own_wts[...])

    def build(g, _):
        at = pl.ds(pl.multiple_of(g * per, per), per)
        high, weight = hi_at[at, :], weight_at[at, :]
        low = jnp.sum(lo_at[at, :], 0, keepdims=True)
        spans = leads + leads % 2
        left = jnp.concatenate(
            [jnp.where(high == float(i), weight, 0.0) for i in range(spans)], 0
        ).astype(jnp.bfloat16)
        digits = lax.broadcasted_iota(jnp.int32, (radix, radix), 0).astype(jnp.float32)
        right = jnp.where(digits == low, 1.0, 0.0).astype(jnp.bfloat16)
        made = lax.dot_general(
            left, right, (((1,), (1,)), ((), ())), preferred_element_type=jnp.float32
        )
        for i in range(leads):
            table[at, i * radix:(i + 1) * radix] = made[i * per:(i + 1) * per]
        return 0

    lax.fori_loop(0, queries // per, build, 0)

    def arrive(t, _):
        for j in range(len(across)):
            share_copy(j, t).wait()
        return 0

    lax.fori_loop(0, tiles, arrive, 0)

    total = jnp.zeros((2 * docs * pad, queries), jnp.float32)
    for t in range(tiles):
        value = slots[:, t].reshape(docs * pad, tile)
        top = value.astype(jnp.bfloat16)
        rest = (value - top.astype(jnp.float32)).astype(jnp.bfloat16)
        pair = jnp.concatenate([top, rest], 0)
        weight = table[:, t * tile:(t + 1) * tile]
        big = weight.astype(jnp.bfloat16)
        small = (weight - big.astype(jnp.float32)).astype(jnp.bfloat16)
        for piece in (big, small):
            total = total + lax.dot_general(
                pair, piece, (((1,), (1,)), ((), ())), preferred_element_type=jnp.float32
            )
    total = (total[:docs * pad] + total[docs * pad:]) * score_scale
    part[...] = total.reshape(docs, pad, queries)

    share = docs // vocs
    copies = []
    for j, peer in enumerate(along):
        copy = pltpu.make_async_remote_copy(
            src_ref=part.at[pl.ds(peer[2] * share, share)], dst_ref=parts.at[j],
            send_sem=voc_send.at[j], recv_sem=voc_recv.at[j], device_id=peer,
            device_id_type=mesh_ids
        )
        copy.start()
        copies.append(copy)
    result = part[pl.ds(voc * share, share)]
    for j, copy in enumerate(copies):
        copy.wait()
        result = result + parts[j]
    for i in range(share):
        out[i * count:(i + 1) * count, :] = result[i, :count]


def shards(
    hidden, lengths, w_trans, b_trans, ln_gain, ln_bias, w_decode, b_decode, query_ids, query_wts
):
    docs, vocs = lax.axis_size("doc"), lax.axis_size("voc")
    count, length, features = hidden.shape
    width = w_decode.shape[1]
    tile = tile_of(width)
    tiles = width // tile
    terms = query_ids.shape[1]
    queries = query_ids.shape[0] // docs
    anywhere = pl.BlockSpec(memory_space=pl.ANY)
    inside = pl.BlockSpec(memory_space=pltpu.VMEM)
    lanes = pltpu.VMEM((queries, radix), jnp.float32)
    queue = pltpu.SemaphoreType.DMA
    return pl.pallas_call(
        functools.partial(encode_kernel, (docs, vocs), count, tile),
        out_shape=jax.ShapeDtypeStruct((docs * count // vocs, queries), jnp.float32),
        in_specs=[pl.BlockSpec(memory_space=pltpu.SMEM)] + [inside] * 4 + [anywhere] * 5,
        out_specs=inside,
        scratch_shapes=[
            pltpu.VMEM((count * length, features), jnp.bfloat16),
            pltpu.VMEM((features, features), jnp.bfloat16),
            pltpu.VMEM((tiles, features, tile), jnp.bfloat16),
            pltpu.VMEM((count * length, features), jnp.bfloat16),
            pltpu.VMEM((docs, tiles, pad, tile), jnp.float32),
            pltpu.VMEM((terms, queries), jnp.int32),
            pltpu.VMEM((terms, queries), jnp.int32),
            lanes, lanes, lanes,
            pltpu.VMEM((queries, width), jnp.float32),
            pltpu.VMEM((docs, pad, queries), jnp.float32),
            pltpu.VMEM((vocs - 1, docs // vocs, pad, queries), jnp.float32),
            queue((3,)), queue((count,)), queue((tiles,)),
            queue((docs - 1, tiles)), queue((docs - 1, tiles)),
            queue((vocs - 1,)), queue((vocs - 1,)),
        ],
        compiler_params=pltpu.CompilerParams(
            collective_id=0, has_side_effects=True, vmem_limit_bytes=60 * 1024 * 1024
        ),
    )(
        lengths, b_trans, ln_gain, ln_bias, b_decode,
        hidden.reshape(count * length, features), w_trans, w_decode, query_ids.T, query_wts.T
    )


def solution(mesh):
    return jax.shard_map(
        shards,
        mesh=mesh,
        in_specs=(
            P(("grp", "doc"), None, None),
            P(("grp", "doc")),
            P(),
            P(),
            P(),
            P(),
            P(None, "voc"),
            P("voc"),
            P("grp", None),
            P("grp", None),
        ),
        out_specs=P(("grp", "voc"), "doc"),
        check_vma=False,
    )
```

```python
import functools

import jax
import jax.numpy as jnp
from jax import lax
from jax.experimental import pallas as pl
from jax.experimental.pallas import tpu as pltpu
from jax.sharding import PartitionSpec as P

eps = 1e-06
score_scale = 1.0 / 1024.0
radix = 256
pad = 8


def tile_of(width):
    best = 128
    for tile in range(128, 1537, 128):
        if width % tile == 0:
            best = tile
    return best


def encode_kernel(
    sizes, count, tile, lens, b_trans, gain, bias, b_decode, hidden, w_trans, w_decode, ids, wts,
    out, states, mix, decoder, kept, slots, own_ids, own_wts, hi_at, lo_at, weight_at, table,
    part, parts, load_sem, state_sem, decoder_sem, doc_send, doc_recv, voc_send, voc_recv
):
    docs, vocs = sizes
    length, features = hidden.shape[0] // count, hidden.shape[1]
    width = w_decode.shape[1]
    tiles = width // tile
    slots_per, queries = own_ids.shape
    per = radix // slots_per
    leads = width // radix
    grp, doc, voc = (lax.axis_index(name) for name in ("grp", "doc", "voc"))
    mesh_ids = pl.DeviceIdType.MESH

    def state_load(p):
        rows = pl.ds(pl.multiple_of(p * length, length), length)
        return pltpu.make_async_copy(hidden.at[rows], states.at[rows], state_sem.at[p])

    def decoder_load(t):
        cut = pl.ds(pl.multiple_of(t * tile, tile), tile)
        return pltpu.make_async_copy(w_decode.at[:, cut], decoder.at[t], decoder_sem.at[t])

    mix_load = pltpu.make_async_copy(w_trans, mix, load_sem.at[0])
    mix_load.start()
    for p in range(count):
        state_load(p).start()
    rows = pl.ds(pl.multiple_of(doc * queries, queries), queries)
    loads = [
        pltpu.make_async_copy(ids.at[:, rows], own_ids, load_sem.at[1]),
        pltpu.make_async_copy(wts.at[:, rows], own_wts, load_sem.at[2]),
    ]
    for load in loads:
        load.start()
    for t in range(tiles):
        decoder_load(t).start()

    barrier = pltpu.get_barrier_semaphore()
    across = [(grp, lax.rem(doc + j, docs), voc) for j in range(1, docs)]
    along = [(grp, doc, lax.rem(voc + j, vocs)) for j in range(1, vocs)]
    for peer in across + along:
        pl.semaphore_signal(barrier, inc=1, device_id=peer, device_id_type=mesh_ids)
    mix_load.wait()

    def transform(p, _):
        state_load(p).wait()
        rows = pl.ds(pl.multiple_of(p * length, length), length)
        pre = jnp.dot(states[rows, :], mix[...], preferred_element_type=jnp.float32)
        pre = pre + b_trans[...][None]
        active = 0.5 * pre * (1.0 + lax.erf(pre * (0.5 ** 0.5)))
        centre = active - jnp.mean(active, -1, keepdims=True)
        spread = jnp.mean(centre * centre, -1, keepdims=True)
        normed = centre * lax.rsqrt(spread + eps) * gain[...][None] + bias[...][None]
        inside = lax.broadcasted_iota(jnp.int32, (length, features), 0) < lens[p]
        kept[rows, :] = jnp.where(inside, normed, normed[0:1]).astype(jnp.bfloat16)
        return 0

    lax.fori_loop(0, count, transform, 0)
    pl.semaphore_wait(barrier, len(across) + len(along))

    for load in loads:
        load.wait()
    local = own_ids[...] - voc * width
    lead = jnp.clip(local >> 8, -1, leads)
    spread_to = (
        lax.broadcasted_iota(jnp.int32, (slots_per, radix), 1) % slots_per
        == lax.broadcasted_iota(jnp.int32, (slots_per, radix), 0)
    ).astype(jnp.float32).astype(jnp.bfloat16)

    def widen(value):
        value = value.astype(jnp.float32).astype(jnp.bfloat16)
        return lax.dot_general(
            value, spread_to, (((0,), (0,)), ((), ())), preferred_element_type=jnp.float32
        )

    own = (
        lax.broadcasted_iota(jnp.int32, (queries, radix), 0) % per
        == lax.broadcasted_iota(jnp.int32, (queries, radix), 1) // slots_per
    )
    hi_at[...] = jnp.where(own, widen(lead), -1.0)
    lo_at[...] = jnp.where(own, widen(local & (radix - 1)), 0.0)
    weight_at[...] = widen(own_wts[...])

    def build(g, _):
        at = pl.ds(pl.multiple_of(g * per, per), per)
        high, weight = hi_at[at, :], weight_at[at, :]
        low = jnp.sum(lo_at[at, :], 0, keepdims=True)
        spans = leads + leads % 2
        left = jnp.concatenate(
            [jnp.where(high == float(i), weight, 0.0) for i in range(spans)], 0
        ).astype(jnp.bfloat16)
        digits = lax.broadcasted_iota(jnp.int32, (radix, radix), 0).astype(jnp.float32)
        right = jnp.where(digits == low, 1.0, 0.0).astype(jnp.bfloat16)
        made = lax.dot_general(
            left, right, (((1,), (1,)), ((), ())), preferred_element_type=jnp.float32
        )
        for i in range(leads):
            table[at, i * radix:(i + 1) * radix] = made[i * per:(i + 1) * per]
        return 0

    groups = queries // per
    inner = groups * 5 // 8 // tiles

    def share_copy(j, t):
        mine = slots.at[doc, t]
        return pltpu.make_async_remote_copy(
            src_ref=mine, dst_ref=mine, send_sem=doc_send.at[j, t], recv_sem=doc_recv.at[j, t],
            device_id=across[j], device_id_type=mesh_ids
        )

    def decode(t, _):
        decoder_load(t).wait()
        for i in range(inner):
            build(t * inner + i, 0)
        tops = []
        for p in range(count):
            logits = jnp.dot(
                kept[p * length:(p + 1) * length, :], decoder[t],
                preferred_element_type=jnp.float32
            )
            tops.append(jnp.max(logits, 0, keepdims=True))
        tops.append(jnp.zeros((pad - count, tile), jnp.float32))
        cut = pl.ds(pl.multiple_of(t * tile, tile), tile)
        best = jnp.concatenate(tops, 0) + b_decode[cut][None]
        slots[doc, t] = jnp.log1p(jnp.maximum(best, 0.0))
        for j in range(len(across)):
            share_copy(j, t).start()
        return 0

    lax.fori_loop(0, tiles, decode, 0)

    lax.fori_loop(inner * tiles, groups, build, 0)

    def arrive(t, _):
        for j in range(len(across)):
            share_copy(j, t).wait()
        return 0

    lax.fori_loop(0, tiles, arrive, 0)

    total = jnp.zeros((2 * docs * pad, queries), jnp.float32)
    for t in range(tiles):
        value = slots[:, t].reshape(docs * pad, tile)
        top = value.astype(jnp.bfloat16)
        rest = (value - top.astype(jnp.float32)).astype(jnp.bfloat16)
        pair = jnp.concatenate([top, rest], 0)
        weight = table[:, t * tile:(t + 1) * tile]
        big = weight.astype(jnp.bfloat16)
        small = (weight - big.astype(jnp.float32)).astype(jnp.bfloat16)
        for piece in (big, small):
            total = total + lax.dot_general(
                pair, piece, (((1,), (1,)), ((), ())), preferred_element_type=jnp.float32
            )
    total = (total[:docs * pad] + total[docs * pad:]) * score_scale
    part[...] = total.reshape(docs, pad, queries)

    share = docs // vocs
    copies = []
    for j, peer in enumerate(along):
        copy = pltpu.make_async_remote_copy(
            src_ref=part.at[pl.ds(peer[2] * share, share)], dst_ref=parts.at[j],
            send_sem=voc_send.at[j], recv_sem=voc_recv.at[j], device_id=peer,
            device_id_type=mesh_ids
        )
        copy.start()
        copies.append(copy)
    result = part[pl.ds(voc * share, share)]
    for j, copy in enumerate(copies):
        copy.wait()
        result = result + parts[j]
    for i in range(share):
        out[i * count:(i + 1) * count, :] = result[i, :count]


def shards(
    hidden, lengths, w_trans, b_trans, ln_gain, ln_bias, w_decode, b_decode, query_ids, query_wts
):
    docs, vocs = lax.axis_size("doc"), lax.axis_size("voc")
    count, length, features = hidden.shape
    width = w_decode.shape[1]
    tile = tile_of(width)
    tiles = width // tile
    terms = query_ids.shape[1]
    queries = query_ids.shape[0] // docs
    anywhere = pl.BlockSpec(memory_space=pl.ANY)
    inside = pl.BlockSpec(memory_space=pltpu.VMEM)
    lanes = pltpu.VMEM((queries, radix), jnp.float32)
    queue = pltpu.SemaphoreType.DMA
    return pl.pallas_call(
        functools.partial(encode_kernel, (docs, vocs), count, tile),
        out_shape=jax.ShapeDtypeStruct((docs * count // vocs, queries), jnp.float32),
        in_specs=[pl.BlockSpec(memory_space=pltpu.SMEM)] + [inside] * 4 + [anywhere] * 5,
        out_specs=inside,
        scratch_shapes=[
            pltpu.VMEM((count * length, features), jnp.bfloat16),
            pltpu.VMEM((features, features), jnp.bfloat16),
            pltpu.VMEM((tiles, features, tile), jnp.bfloat16),
            pltpu.VMEM((count * length, features), jnp.bfloat16),
            pltpu.VMEM((docs, tiles, pad, tile), jnp.float32),
            pltpu.VMEM((terms, queries), jnp.int32),
            pltpu.VMEM((terms, queries), jnp.int32),
            lanes, lanes, lanes,
            pltpu.VMEM((queries, width), jnp.float32),
            pltpu.VMEM((docs, pad, queries), jnp.float32),
            pltpu.VMEM((vocs - 1, docs // vocs, pad, queries), jnp.float32),
            queue((3,)), queue((count,)), queue((tiles,)),
            queue((docs - 1, tiles)), queue((docs - 1, tiles)),
            queue((vocs - 1,)), queue((vocs - 1,)),
        ],
        compiler_params=pltpu.CompilerParams(
            collective_id=0, has_side_effects=True, vmem_limit_bytes=60 * 1024 * 1024
        ),
    )(
        lengths, b_trans, ln_gain, ln_bias, b_decode,
        hidden.reshape(count * length, features), w_trans, w_decode, query_ids.T, query_wts.T
    )


def solution(mesh):
    return jax.shard_map(
        shards,
        mesh=mesh,
        in_specs=(
            P(("grp", "doc"), None, None),
            P(("grp", "doc")),
            P(),
            P(),
            P(),
            P(),
            P(None, "voc"),
            P("voc"),
            P("grp", None),
            P("grp", None),
        ),
        out_specs=P(("grp", "voc"), "doc"),
        check_vma=False,
    )
```
